32 devices in a mesh: dp: 8 (over y, x, core), tensor: 4 (over z).
Axes of the slice: x: 2, y: 2, z: 4, core: 2. Of those that a mesh axis runs over, the one named last changes fastest.
Arguments:
- tokens: bfloat16 [8192, 2048], P(('dp', 'tensor')), may hold values from -6 to 6
- w_qkv: float32 [3, 2048, 2048], P(None, 'dp', 'tensor'), may hold values from -0.125 to 0.125
- w_out: float32 [2048, 2048], P('tensor', 'dp'), may hold values from -0.5 to 0.5
- w_up: float32 [2048, 8192], P('dp', 'tensor'), may hold values from -0.125 to 0.125
- w_down: float32 [8192, 2048], P('tensor', 'dp'), may hold values from -0.0625 to 0.0625
- norm_gains: float32 [2, 2048], P(None, 'dp'), may hold values from 0.25 to 1.75
- norm_biases: float32 [2, 2048], P(None, 'dp'), may hold values from -1.75 to 1.75
- lengths: int32 [8], P('dp'), may hold values from 256 to 1024, as said below
- cotangent: bfloat16 [8192, 2048], P(('dp', 'tensor')), may hold values from -6 to 6
Outputs:
- output: bfloat16 [8192, 2048], P(('dp', 'tensor'))
- input_grad: bfloat16 [8192, 2048], P(('dp', 'tensor'))
- grad_qkv: float32 [3, 2048, 2048], P(None, 'dp', 'tensor')
- grad_out: float32 [2048, 2048], P('tensor', 'dp')
- grad_up: float32 [2048, 8192], P('dp', 'tensor')
- grad_down: float32 [8192, 2048], P('tensor', 'dp')
- gain_grads: float32 [2, 2048], P(None, ('dp', 'tensor'))
- bias_grads: float32 [2, 2048], P(None, ('dp', 'tensor'))
The draws below stay inside these ranges and needn't reach their ends.
Inputs may be any that keep to these rules, and one draw needn't show every extreme that they name: `lengths`: one sequence has exactly 1024 valid slots and one exactly 256.
All inputs are finite; a program needn't handle non-finite values.
Results may differ from the reference program's by a relative error of at most 0.019.
Values may be sent and summed in bfloat16 or wider, within the bound.
A program may use at most 192 MiB of HBM per device.

```python
import math
import jax
import jax.numpy as jnp
from jax import lax

D = 2048
HEADS = 32
HEAD_DIM = 64
FF = 8192
SEQ_LEN = 1024
BLOCK = 512
LEN_MIN = 256
SEQS = 8
TOKENS = 8192


def draw_lengths(key, part):
    base = jax.random.randint(key, (SEQS,), LEN_MIN, SEQ_LEN + 1, dtype=jnp.int32)
    full_slot = jax.random.randint(jax.random.fold_in(key, 1), (), 0, SEQS, dtype=jnp.int32)
    offset = jax.random.randint(jax.random.fold_in(key, 2), (), 1, SEQS, dtype=jnp.int32)
    short_slot = (full_slot + offset) % SEQS
    slots = jnp.arange(SEQS, dtype=jnp.int32)
    base = jnp.where(slots == full_slot, SEQ_LEN, base)
    return jnp.where(slots == short_slot, LEN_MIN, base).astype(jnp.int32)


def levels(stream_key, shape, shards, least, high):
    factor_of, own = 1.0, jax.random.fold_in(stream_key, 6)
    for position, shards_of in shards:
        steps = jnp.exp(jax.random.uniform(jax.random.fold_in(own, position), (shards_of,), jnp.float32, least / len(shards), high / len(shards)))
        factor_of = factor_of * jnp.repeat(steps, shape[position] // shards_of).reshape([-1 if axis == position else 1 for axis in range(len(shape))])
    return factor_of


def normal_values(stream_key, extent, scale, limit, split=(), held_as=jnp.bfloat16):
    drawn = jax.random.normal(stream_key, extent, jnp.float32) * scale
    if len(split) > 0:
        drawn = levels(stream_key, extent, split, -0.22, 0.18) * drawn
    return jnp.clip(drawn, min=-limit, max=limit).astype(held_as)


def setup_inputs(seed: int = 0) -> dict:
    splits = jax.random.split(jax.random.key(seed), 10)
    return {
        "tokens": normal_values(splits[0], (TOKENS, D), 1.0, 6.0, ((0, 32),)),
        "w_qkv": normal_values(splits[1], (3, D, D), D ** -0.5, 0.125, ((1, 8), (2, 4)), jnp.float32),
        "w_out": normal_values(splits[2], (D, D), (D // 16) ** -0.5, 0.5, ((0, 4), (1, 8)), jnp.float32),
        "w_up": normal_values(splits[3], (D, FF), D ** -0.5, 0.125, ((0, 8), (1, 4)), jnp.float32),
        "w_down": normal_values(splits[4], (FF, D), FF ** -0.5, 0.0625, ((0, 4), (1, 8)), jnp.float32),
        "norm_gains": jnp.clip(1.0 + 0.15 * jax.random.normal(splits[5], (2, D), jnp.float32), 0.25, 1.75),
        "norm_biases": normal_values(splits[6], (2, D), 0.3, 1.75, ((1, 8),), jnp.float32),
        "lengths": draw_lengths(jax.random.fold_in(splits[9], 71), 0),
        "cotangent": normal_values(splits[8], (TOKENS, D), 1.0, 6.0, ((0, 32),)),
    }


EPSILON = 1e-05
MASKED = -1e+30
HIGHEST = lax.Precision.HIGHEST

@jax.custom_vjp
def low(v):
    return lax.optimization_barrier(v.astype(jnp.bfloat16)).astype(jnp.float32)

@jax.custom_vjp
def low_back(v):
    return v

def low_keep(v):
    return (low(v), None)

def low_pass(kept, grad):
    return (grad,)

def back_keep(v):
    return (v, None)

def back_low(kept, grad):
    return (low(grad),)
low.defvjp(low_keep, low_pass)
low_back.defvjp(back_keep, back_low)

def mat_high(left, right):
    return jnp.dot(left, right, precision=HIGHEST, preferred_element_type=jnp.float32)

def layer_norm(values, gain, shift):
    center = lax.optimization_barrier(jnp.mean(values, axis=-1, keepdims=True))
    offset = values - center
    spread = lax.optimization_barrier(jnp.mean(offset * offset, axis=-1, keepdims=True))
    return offset * lax.rsqrt(spread + EPSILON) * gain + shift

def alibi_slopes():
    head_ids = jnp.arange(HEADS).astype(jnp.float32)
    return jnp.exp2(-8.0 * (head_ids + 1.0) / HEADS)

def attend(queries, keys_all, values_all, length):
    slopes = alibi_slopes()
    key_pos = jnp.arange(SEQ_LEN).astype(jnp.int32)
    scale = 1.0 / math.sqrt(HEAD_DIM)

    def one_block(blk_start):
        query_blk = lax.dynamic_slice_in_dim(queries, blk_start, BLOCK, 0)
        row_pos = blk_start + jnp.arange(BLOCK).astype(jnp.int32)
        scores = jnp.einsum('qhd,khd->hqk', query_blk, keys_all, precision=HIGHEST) * scale
        distance = (row_pos[:, None] - key_pos[None, :]).astype(jnp.float32)
        scores = scores - slopes[:, None, None] * distance[None]
        scores = low_back(scores)
        allowed = (key_pos[None, :] <= row_pos[:, None]) & (key_pos[None, :] < length)
        scores = jnp.where(allowed[None], scores, MASKED)
        row_top = lax.optimization_barrier(jnp.max(scores, axis=-1, keepdims=True))
        weights = jnp.exp(scores - row_top)
        row_probs = weights / lax.optimization_barrier(jnp.sum(weights, axis=-1, keepdims=True))
        return jnp.einsum('hqk,khd->qhd', low(row_probs), values_all, precision=HIGHEST)
    starts = (jnp.arange(SEQ_LEN // BLOCK) * BLOCK).astype(jnp.int32)
    blocks = lax.map(jax.checkpoint(one_block), starts)
    return blocks.reshape(SEQ_LEN, HEADS * HEAD_DIM)

def block_layer(inputs, w_qkv, w_out, w_up, w_down, norm_gains, norm_biases, length):
    gains = low(norm_gains)
    shifts = low(norm_biases)
    normed_one = low(layer_norm(inputs, gains[0], shifts[0]))
    qkv_weights = low(w_qkv)
    queries = low(low_back(mat_high(normed_one, qkv_weights[0])))
    keys_all = low(low_back(mat_high(normed_one, qkv_weights[1])))
    values_all = low(low_back(mat_high(normed_one, qkv_weights[2])))
    mixed = attend(queries.reshape(SEQ_LEN, HEADS, HEAD_DIM), keys_all.reshape(SEQ_LEN, HEADS, HEAD_DIM), values_all.reshape(SEQ_LEN, HEADS, HEAD_DIM), length)
    mixed = low(low_back(mixed))
    after_attn = inputs + low_back(mat_high(mixed, low(w_out)))
    normed_two = low(layer_norm(after_attn, gains[1], shifts[1]))
    pre_act = low_back(mat_high(normed_two, low(w_up)))
    activated = low(jax.nn.gelu(pre_act, approximate=False))
    result = after_attn + low_back(mat_high(activated, low(w_down)))
    live_rows = jnp.arange(SEQ_LEN).astype(jnp.int32) < length
    return jnp.where(live_rows[:, None], result, 0.0)

def reference(tokens, w_qkv, w_out, w_up, w_down, norm_gains, norm_biases, lengths, cotangent):
    inputs = tokens.astype(jnp.float32).reshape(SEQS, SEQ_LEN, D)
    cotangents = cotangent.astype(jnp.float32).reshape(SEQS, SEQ_LEN, D)
    params = (w_qkv, w_out, w_up, w_down, norm_gains, norm_biases)

    def one_sequence(running, per_seq):
        seq_in, seq_cot, length = per_seq

        def apply_layer(seq_values, *weights):
            return block_layer(seq_values, *weights, length)
        result, pullback = jax.vjp(apply_layer, seq_in, *params)
        gradients = pullback(seq_cot)
        running = tuple((acc + part for acc, part in zip(running, gradients[1:])))
        return (running, (result, gradients[0]))
    zeros = tuple((jnp.zeros_like(param) for param in params))
    running, (outputs, input_grads) = lax.scan(one_sequence, zeros, (inputs, cotangents, lengths))
    return (outputs.reshape(TOKENS, D).astype(jnp.bfloat16), input_grads.reshape(TOKENS, D).astype(jnp.bfloat16), running[0], running[1], running[2], running[3], running[4], running[5])
```

```python
import functools

import jax
import jax.numpy as jnp
from jax import lax
from jax.experimental import pallas as pl
from jax.experimental.pallas import tpu as pltpu
from jax.sharding import PartitionSpec as P

HEAD_DIM = 64
LANES = 128
TILE = 256
PARTS = 4
VMEM_BYTES = 60 * 1024 * 1024

EPSILON = 1e-05
MASKED = -1e30
INV_ROOT_TAU = 0.3989422804014327
ROOT_HALF = 0.7071067811865476

MESH = pl.DeviceIdType.MESH
ANY = pl.BlockSpec(memory_space=pl.ANY)
F32 = jnp.float32
BF16 = jnp.bfloat16


def dot_nn(left, right):
    return lax.dot_general(left, right, (((1,), (0,)), ((), ())), preferred_element_type=F32)


def dot_nt(left, right):
    return lax.dot_general(left, right, (((1,), (1,)), ((), ())), preferred_element_type=F32)


def dot_tn(left, right):
    return lax.dot_general(left, right, (((0,), (0,)), ((), ())), preferred_element_type=F32)


def normalize(values):
    center = jnp.mean(values, axis=-1, keepdims=True)
    offset = values - center
    spread = jnp.mean(offset * offset, axis=-1, keepdims=True)
    inv_std = lax.rsqrt(spread + EPSILON)
    return (offset * inv_std, inv_std)


def norm_back(grads, normed, inv_std, gain):
    scaled = grads * gain
    return inv_std * (
        scaled
        - jnp.mean(scaled, axis=-1, keepdims=True)
        - normed * jnp.mean(scaled * normed, axis=-1, keepdims=True)
    )


def block_at(index, size):
    return pl.ds(pl.multiple_of(index * size, size), size)


def line_enter(p, n):
    barrier = pltpu.get_barrier_semaphore()

    @pl.when(p > 0)
    def _():
        pl.semaphore_signal(barrier, inc=1, device_id={"tensor": p - 1}, device_id_type=MESH)

    @pl.when(p < n - 1)
    def _():
        pl.semaphore_signal(barrier, inc=1, device_id={"tensor": p + 1}, device_id_type=MESH)

    pl.semaphore_wait(barrier, jnp.where(p > 0, 1, 0) + jnp.where(p < n - 1, 1, 0))


class Line:
    def __init__(self, n, rows):
        self.n = n
        self.p = lax.axis_index("tensor")
        self.rows = rows
        self.piece = rows // PARTS
        self.right = lax.rem(self.p + 1, n)
        self.left = lax.rem(self.p + n - 1, n)

    def slot(self, ref, j, c):
        start = pl.multiple_of(j * self.rows + c * self.piece, self.piece)
        return ref.at[pl.ds(start, self.piece)]

    def shard(self, ref, j):
        return ref.at[block_at(j, self.rows)]


class Gather:
    def __init__(self, line, buf, right_sem, left_sem, recv_sem):
        self.line, self.buf = line, buf
        self.right_sem, self.left_sem, self.recv_sem = right_sem, left_sem, recv_sem

    def copy(self, j, c, rightward):
        line = self.line
        slot = line.slot(self.buf, j, c)
        i = j * PARTS + c
        return pltpu.make_async_remote_copy(
            src_ref=slot,
            dst_ref=slot,
            send_sem=(self.right_sem if rightward else self.left_sem).at[i],
            recv_sem=self.recv_sem.at[i],
            device_id={"tensor": line.right if rightward else line.left},
            device_id_type=MESH,
        )

    def begin(self):
        p, n = self.line.p, self.line.n
        for c in range(PARTS):

            @pl.when(p < n - 1)
            def _():
                self.copy(p, c, True).start()

            @pl.when(p > 0)
            def _():
                self.copy(p, c, False).start()

    def step(self, s, c):
        p, n = self.line.p, self.line.n

        @pl.when(p - s >= 0)
        def _():
            copy = self.copy(p - s, c, True)
            copy.wait_recv()

            @pl.when(p < n - 1)
            def _():
                copy.start()

        @pl.when(p + s < n)
        def _():
            copy = self.copy(p + s, c, False)
            copy.wait_recv()

            @pl.when(p > 0)
            def _():
                copy.start()

    def end(self):
        p, n = self.line.p, self.line.n

        @pl.loop(0, n)
        def _(j):
            for c in range(PARTS):

                @pl.when((j <= p) & (p < n - 1))
                def _():
                    self.copy(j, c, True).wait_send()

                @pl.when((j >= p) & (p > 0))
                def _():
                    self.copy(j, c, False).wait_send()


class Scatter:
    def __init__(self, line, part, from_left, from_right, right_sem, left_sem, lrecv_sem, rrecv_sem):
        self.line, self.part, self.from_left, self.from_right = line, part, from_left, from_right
        self.right_sem, self.left_sem = right_sem, left_sem
        self.lrecv_sem, self.rrecv_sem = lrecv_sem, rrecv_sem

    def copy(self, j, c, rightward):
        line = self.line
        i = j * PARTS + c
        return pltpu.make_async_remote_copy(
            src_ref=line.slot(self.part, j, c),
            dst_ref=line.slot(self.from_left if rightward else self.from_right, j, c),
            send_sem=(self.right_sem if rightward else self.left_sem).at[i],
            recv_sem=(self.lrecv_sem if rightward else self.rrecv_sem).at[i],
            device_id={"tensor": line.right if rightward else line.left},
            device_id_type=MESH,
        )

    def add(self, j, c, ref):
        part = self.line.slot(self.part, j, c)
        total = part[...].astype(F32) + self.line.slot(ref, j, c)[...].astype(F32)
        part[...] = total.astype(BF16)

    def send_right(self, j, c):
        p, n = self.line.p, self.line.n

        @pl.when((j > p) & (j < n))
        def _():
            copy = self.copy(j, c, True)

            @pl.when(p > 0)
            def _():
                copy.wait_recv()
                self.add(j, c, self.from_left)

            copy.start()

    def send_left(self, j, c):
        p, n = self.line.p, self.line.n

        @pl.when((j < p) & (j >= 0))
        def _():
            copy = self.copy(j, c, False)

            @pl.when(p < n - 1)
            def _():
                copy.wait_recv()
                self.add(j, c, self.from_right)

            copy.start()

    def finish(self, out):
        p, n = self.line.p, self.line.n
        piece = self.line.piece
        for c in range(PARTS):
            mine = out.at[pl.ds(c * piece, piece)]
            mine[...] = self.line.slot(self.part, p, c)[...].astype(F32)

            @pl.when(p > 0)
            def _():
                self.copy(p, c, True).wait_recv()
                mine[...] += self.line.slot(self.from_left, p, c)[...].astype(F32)

            @pl.when(p < n - 1)
            def _():
                self.copy(p, c, False).wait_recv()
                mine[...] += self.line.slot(self.from_right, p, c)[...].astype(F32)

    def end(self):
        p, n = self.line.p, self.line.n

        @pl.loop(0, n)
        def _(j):
            for c in range(PARTS):

                @pl.when(j > p)
                def _():
                    self.copy(j, c, True).wait_send()

                @pl.when(j < p)
                def _():
                    self.copy(j, c, False).wait_send()


def line_sems(n):
    return pltpu.SemaphoreType.DMA((n * PARTS,))


def remote_call(body, name, collective_id, outs, scratch, micros, *args):
    return pl.pallas_call(
        body,
        name=name,
        out_shape=outs,
        in_specs=[ANY] * len(args),
        out_specs=jax.tree.map(lambda _: ANY, outs),
        scratch_shapes=scratch,
        cost_estimate=pl.CostEstimate(
            flops=int(micros * 1e-6 * 1.15e15), bytes_accessed=1 << 20, transcendentals=0
        ),
        compiler_params=pltpu.CompilerParams(
            collective_id=collective_id, has_side_effects=True, vmem_limit_bytes=VMEM_BYTES
        ),
    )(*args)


def project_kernel(
    n, rows, h_ref, w_ref, qkv_ref, all_ref, buf, w_v, o_v, right_sem, left_sem, recv_sem, load_sem, q_sem, h_sem
):
    line = Line(n, rows)
    p = line.p
    width = w_v.shape[2]
    load_w = pltpu.make_async_copy(w_ref, w_v, load_sem.at[0])
    load_h = pltpu.make_async_copy(h_ref, line.shard(buf, p), load_sem.at[1])
    load_h.start()
    load_w.start()
    line_enter(p, n)
    load_h.wait()
    gather = Gather(line, buf, right_sem, left_sem, recv_sem)
    gather.begin()

    def stores(j):
        at = block_at(j, rows)
        return (
            pltpu.make_async_copy(o_v.at[:, at], qkv_ref.at[:, at], q_sem.at[j]),
            pltpu.make_async_copy(buf.at[at], all_ref.at[at], h_sem.at[j]),
        )

    def compute(j):
        at = block_at(j, rows)
        for i in range(3):

            @pl.loop(0, width // TILE)
            def _(t):
                cols = block_at(t, TILE)
                o_v[i, at, cols] = dot_nn(buf[at, :], w_v[i, :, cols]).astype(BF16)

        for copy in stores(j):
            copy.start()

    load_w.wait()
    compute(p)

    @pl.loop(1, n)
    def _(s):
        for c in range(PARTS):
            gather.step(s, c)

        @pl.when(p - s >= 0)
        def _():
            compute(p - s)

        @pl.when(p + s < n)
        def _():
            compute(p + s)

    gather.end()

    @pl.loop(0, n)
    def _(j):
        for copy in stores(j):
            copy.wait()


def project(normed, weights, n):
    rows, model = normed.shape
    width = weights.shape[2]
    group = n * rows
    return remote_call(
        functools.partial(project_kernel, n, rows),
        "project",
        1,
        (jax.ShapeDtypeStruct((3, group, width), BF16), jax.ShapeDtypeStruct((group, model), BF16)),
        [
            pltpu.VMEM((group, model), BF16),
            pltpu.VMEM(weights.shape, BF16),
            pltpu.VMEM((3, group, width), BF16),
            line_sems(n),
            line_sems(n),
            line_sems(n),
            pltpu.SemaphoreType.DMA((2,)),
            pltpu.SemaphoreType.DMA((n,)),
            pltpu.SemaphoreType.DMA((n,)),
        ],
        78,
        normed,
        weights,
    )


def branch_kernel(
    n, rows, attn_ref, w_ref, g_ref, out_ref, all_ref,
    a_v, w_v, buf, part, from_left, from_right, out_v,
    gr_sem, gl_sem, grecv_sem, sr_sem, sl_sem, lrecv_sem, rrecv_sem, load_sem, store_sem,
):
    line = Line(n, rows)
    p = line.p
    model = w_v.shape[1]
    loads = (
        pltpu.make_async_copy(g_ref, line.shard(buf, p), load_sem.at[0]),
        pltpu.make_async_copy(attn_ref, a_v, load_sem.at[1]),
        pltpu.make_async_copy(w_ref, w_v, load_sem.at[2]),
    )
    for copy in loads:
        copy.start()
    line_enter(p, n)
    for copy in loads:
        copy.wait()
    gather = Gather(line, buf, gr_sem, gl_sem, grecv_sem)
    scatter = Scatter(line, part, from_left, from_right, sr_sem, sl_sem, lrecv_sem, rrecv_sem)
    gather.begin()

    def compute(j):
        at = block_at(j, rows)

        @pl.loop(0, model // TILE)
        def _(t):
            cols = block_at(t, TILE)
            part[at, cols] = dot_nn(a_v[at, :], w_v[:, cols]).astype(BF16)

    @pl.loop(0, n)
    def _(s):
        right, left = n - 1 - s, s

        @pl.when(right > p)
        def _():
            compute(right)

        @pl.when(left < p)
        def _():
            compute(left)

        for c in range(PARTS):
            scatter.send_right(right, c)
            scatter.send_left(left, c)

            @pl.when(s + 1 < n)
            def _():
                gather.step(s + 1, c)

    compute(p)
    scatter.finish(out_v)
    stores = (
        pltpu.make_async_copy(out_v, out_ref, store_sem.at[0]),
        pltpu.make_async_copy(buf, all_ref, store_sem.at[1]),
    )
    for copy in stores:
        copy.start()
    scatter.end()
    gather.end()
    for copy in stores:
        copy.wait()


def branch(attn, w_out, cot, n):
    rows, model = cot.shape
    group = n * rows
    full = pltpu.VMEM((group, model), BF16)
    return remote_call(
        functools.partial(branch_kernel, n, rows),
        "branch",
        2,
        (jax.ShapeDtypeStruct((rows, model), F32), jax.ShapeDtypeStruct((group, model), BF16)),
        [
            pltpu.VMEM(attn.shape, BF16),
            pltpu.VMEM(w_out.shape, BF16),
            full, full, full, full,
            pltpu.VMEM((rows, model), F32),
        ]
        + [line_sems(n)] * 7
        + [pltpu.SemaphoreType.DMA((3,)), pltpu.SemaphoreType.DMA((2,))],
        100,
        attn,
        w_out,
        cot,
    )


def feed_kernel(
    n, rows, h_ref, g_ref, up_ref, down_ref, all_ref, act_ref, dup_ref, mlp_ref, dh_ref,
    buf, up_v, down_v, g_v, act_v, dup_v, mlp_v, part, from_left, from_right, out_v,
    gr_sem, gl_sem, grecv_sem, sr_sem, sl_sem, lrecv_sem, rrecv_sem, load_sem, store_sem,
):
    line = Line(n, rows)
    p = line.p
    model, hidden = up_v.shape
    load_h = pltpu.make_async_copy(h_ref, line.shard(buf, p), load_sem.at[0])
    loads = (
        pltpu.make_async_copy(up_ref, up_v, load_sem.at[1]),
        pltpu.make_async_copy(g_ref, g_v, load_sem.at[2]),
        pltpu.make_async_copy(down_ref, down_v, load_sem.at[3]),
    )
    load_h.start()
    for copy in loads:
        copy.start()
    line_enter(p, n)
    load_h.wait()
    gather = Gather(line, buf, gr_sem, gl_sem, grecv_sem)
    scatter = Scatter(line, part, from_left, from_right, sr_sem, sl_sem, lrecv_sem, rrecv_sem)
    gather.begin()
    for copy in loads:
        copy.wait()

    def stores(j):
        at = block_at(j, rows)
        return (
            pltpu.make_async_copy(buf.at[at], all_ref.at[at], store_sem.at[0, j]),
            pltpu.make_async_copy(act_v.at[at], act_ref.at[at], store_sem.at[1, j]),
            pltpu.make_async_copy(dup_v.at[at], dup_ref.at[at], store_sem.at[2, j]),
            pltpu.make_async_copy(mlp_v.at[at], mlp_ref.at[at], store_sem.at[3, j]),
        )

    def compute(j):
        at = block_at(j, rows)

        @pl.loop(0, hidden // TILE)
        def _(t):
            cols = block_at(t, TILE)
            up = dot_nn(buf[at, :], up_v[:, cols])
            d_act = dot_nt(g_v[at, :], down_v[cols, :])
            half = 0.5 * (1.0 + lax.erf(up * ROOT_HALF))
            act_v[at, cols] = (up * half).astype(BF16)
            slope = half + up * jnp.exp(-0.5 * up * up) * INV_ROOT_TAU
            dup_v[at, cols] = (d_act * slope).astype(BF16)

        @pl.loop(0, model // TILE)
        def _(t):
            cols = block_at(t, TILE)
            part[at, cols] = dot_nt(dup_v[at, :], up_v[cols, :]).astype(BF16)

    def compute_down(j):
        at = block_at(j, rows)

        @pl.loop(0, model // TILE)
        def _(t):
            cols = block_at(t, TILE)
            mlp_v[at, cols] = dot_nn(act_v[at, :], down_v[:, cols]).astype(BF16)

        for copy in stores(j):
            copy.start()

    compute(p)
    compute_down(p)

    @pl.loop(1, n)
    def _(s):
        for c in range(PARTS):
            gather.step(s, c)

        @pl.when(p - s >= 0)
        def _():
            compute(p - s)

            @pl.when(p == n - 1)
            def _():
                for c in range(PARTS):
                    scatter.send_left(p - s, c)

            compute_down(p - s)

        @pl.when(p + s < n)
        def _():
            compute(p + s)

            @pl.when(p == 0)
            def _():
                for c in range(PARTS):
                    scatter.send_right(p + s, c)

            compute_down(p + s)

    @pl.loop(1, 2 * n - 2)
    def _(s):
        for c in range(PARTS):

            @pl.when(p > 0)
            def _():
                scatter.send_right(s - p, c)

            @pl.when(p < n - 1)
            def _():
                scatter.send_left(2 * (n - 1) - p - s, c)

    scatter.finish(out_v)
    store_out = pltpu.make_async_copy(out_v, dh_ref, load_sem.at[0])
    store_out.start()
    scatter.end()
    gather.end()

    @pl.loop(0, n)
    def _(j):
        for copy in stores(j):
            copy.wait()

    store_out.wait()


def feed(normed, cot_all, w_up, w_down, n):
    rows, model = normed.shape
    hidden = w_up.shape[1]
    group = n * rows
    full = pltpu.VMEM((group, model), BF16)
    wide = pltpu.VMEM((group, hidden), BF16)
    return remote_call(
        functools.partial(feed_kernel, n, rows),
        "feed",
        3,
        (
            jax.ShapeDtypeStruct((group, model), BF16),
            jax.ShapeDtypeStruct((group, hidden), BF16),
            jax.ShapeDtypeStruct((group, hidden), BF16),
            jax.ShapeDtypeStruct((group, model), BF16),
            jax.ShapeDtypeStruct((rows, model), F32),
        ),
        [
            full,
            pltpu.VMEM(w_up.shape, BF16),
            pltpu.VMEM(w_down.shape, BF16),
            full,
            wide,
            wide,
            full, full, full, full,
            pltpu.VMEM((rows, model), F32),
        ]
        + [line_sems(n)] * 7
        + [pltpu.SemaphoreType.DMA((4,)), pltpu.SemaphoreType.DMA((4, n))],
        140,
        normed,
        cot_all,
        w_up,
        w_down,
    )


def unbranch_kernel(
    n, rows, d_ref, w_ref, mlp_ref, all_ref, da_ref, out_ref,
    buf, w_v, a_v, part, from_left, from_right, out_v,
    gr_sem, gl_sem, grecv_sem, sr_sem, sl_sem, lrecv_sem, rrecv_sem, load_sem, store_sem,
):
    line = Line(n, rows)
    p = line.p
    width, model = w_v.shape
    loads = (
        pltpu.make_async_copy(d_ref, line.shard(buf, p), load_sem.at[0]),
        pltpu.make_async_copy(mlp_ref, part, load_sem.at[1]),
        pltpu.make_async_copy(w_ref, w_v, load_sem.at[2]),
    )
    for copy in loads:
        copy.start()
    line_enter(p, n)
    for copy in loads:
        copy.wait()
    gather = Gather(line, buf, gr_sem, gl_sem, grecv_sem)
    scatter = Scatter(line, part, from_left, from_right, sr_sem, sl_sem, lrecv_sem, rrecv_sem)
    gather.begin()

    def compute(j):
        at = block_at(j, rows)

        @pl.loop(0, width // TILE)
        def _(t):
            cols = block_at(t, TILE)
            a_v[at, cols] = dot_nt(buf[at, :], w_v[cols, :]).astype(BF16)

    @pl.loop(0, n)
    def _(s):
        for c in range(PARTS):

            @pl.when(s > 0)
            def _():
                gather.step(s, c)

            scatter.send_right(n - 1 - s, c)
            scatter.send_left(s, c)

        @pl.when(p - s >= 0)
        def _():
            compute(p - s)

        @pl.when((p + s < n) & (s > 0))
        def _():
            compute(p + s)

    scatter.finish(out_v)
    stores = (
        pltpu.make_async_copy(out_v, out_ref, store_sem.at[0]),
        pltpu.make_async_copy(buf, all_ref, store_sem.at[1]),
        pltpu.make_async_copy(a_v, da_ref, store_sem.at[2]),
    )
    for copy in stores:
        copy.start()
    scatter.end()
    gather.end()
    for copy in stores:
        copy.wait()


def unbranch(d_branch, w_out, mlp_part, n):
    rows, model = d_branch.shape
    group = n * rows
    width = w_out.shape[0]
    full = pltpu.VMEM((group, model), BF16)
    return remote_call(
        functools.partial(unbranch_kernel, n, rows),
        "unbranch",
        4,
        (
            jax.ShapeDtypeStruct((group, model), BF16),
            jax.ShapeDtypeStruct((group, width), BF16),
            jax.ShapeDtypeStruct((rows, model), F32),
        ),
        [
            full,
            pltpu.VMEM(w_out.shape, BF16),
            pltpu.VMEM((group, width), BF16),
            full, full, full,
            pltpu.VMEM((rows, model), F32),
        ]
        + [line_sems(n)] * 7
        + [pltpu.SemaphoreType.DMA((3,)), pltpu.SemaphoreType.DMA((3,))],
        100,
        d_branch,
        w_out,
        mlp_part,
    )


def unproject_kernel(
    n, rows, d_ref, w_ref, out_ref,
    d_v, w_v, part, from_left, from_right, out_v,
    sr_sem, sl_sem, lrecv_sem, rrecv_sem, load_sem,
):
    line = Line(n, rows)
    p = line.p
    model = w_v.shape[1]
    loads = (
        pltpu.make_async_copy(d_ref, d_v, load_sem.at[0]),
        pltpu.make_async_copy(w_ref, w_v, load_sem.at[1]),
    )
    for copy in loads:
        copy.start()
    line_enter(p, n)
    for copy in loads:
        copy.wait()
    scatter = Scatter(line, part, from_left, from_right, sr_sem, sl_sem, lrecv_sem, rrecv_sem)

    def compute(j):
        at = block_at(j, rows)

        @pl.loop(0, model // TILE)
        def _(t):
            cols = block_at(t, TILE)
            total = dot_nt(d_v[0, at, :], w_v[0, cols, :])
            total += dot_nt(d_v[1, at, :], w_v[1, cols, :])
            total += dot_nt(d_v[2, at, :], w_v[2, cols, :])
            part[at, cols] = total.astype(BF16)

    @pl.loop(0, n)
    def _(s):
        right, left = n - 1 - s, s

        @pl.when(right > p)
        def _():
            compute(right)

        @pl.when(left < p)
        def _():
            compute(left)

        for c in range(PARTS):
            scatter.send_right(right, c)
            scatter.send_left(left, c)

    compute(p)
    scatter.finish(out_v)
    store = pltpu.make_async_copy(out_v, out_ref, load_sem.at[0])
    store.start()
    scatter.end()
    store.wait()


def unproject(d_qkv, weights, rows, n):
    model = weights.shape[1]
    group = n * rows
    full = pltpu.VMEM((group, model), BF16)
    return remote_call(
        functools.partial(unproject_kernel, n, rows),
        "unproject",
        5,
        jax.ShapeDtypeStruct((rows, model), F32),
        [
            pltpu.VMEM(d_qkv.shape, BF16),
            pltpu.VMEM(weights.shape, BF16),
            full, full, full,
            pltpu.VMEM((rows, model), F32),
        ]
        + [line_sems(n)] * 4
        + [pltpu.SemaphoreType.DMA((2,))],
        80,
        d_qkv,
        weights,
    )


def fill_bias(bias, slope, length):
    row = lax.broadcasted_iota(jnp.int32, bias.shape, 0)
    bias[...] = jnp.where(row < length, slope * row.astype(F32), MASKED)


def causal_tile():
    shape = (TILE, TILE)
    return lax.broadcasted_iota(jnp.int32, shape, 0) <= lax.broadcasted_iota(jnp.int32, shape, 1)


def attend_kernel(len_ref, slope_ref, q_ref, k_ref, v_ref, out_ref, lse_ref, bias, vt_v):
    pair = pl.program_id(0)
    slots = q_ref.shape[0]
    lane = lax.broadcasted_iota(jnp.int32, (TILE, LANES), 1)
    causal = causal_tile()
    vt_v[...] = v_ref[...].T
    for h in range(2):
        mine = (lane >= HEAD_DIM) if h else (lane < HEAD_DIM)
        fill_bias(bias, slope_ref[pair * 2 + h], len_ref[0])
        for b in range(slots // TILE):
            at = slice(b * TILE, (b + 1) * TILE)
            end = (b + 1) * TILE
            query = jnp.where(mine, q_ref[at, :] * 0.125, 0).astype(BF16)
            last = dot_nt(k_ref[at, :], query) + bias[at, :]
            last = jnp.where(causal, last, MASKED)
            top = jnp.max(last, axis=0, keepdims=True)
            if b > 0:
                first = dot_nt(k_ref[: b * TILE, :], query) + bias[: b * TILE, :]
                top = jnp.maximum(top, jnp.max(first, axis=0, keepdims=True))
            probs = jnp.exp(last - top)
            total = jnp.sum(probs, axis=0, keepdims=True)
            mixed = dot_nn(vt_v[:, at], probs.astype(BF16))
            if b > 0:
                probs = jnp.exp(first - top)
                total += jnp.sum(probs, axis=0, keepdims=True)
                mixed += dot_nn(vt_v[:, : b * TILE], probs.astype(BF16))
            value = (mixed / total).T.astype(BF16)
            if h:
                out_ref[at, :] = jnp.where(mine, value, out_ref[at, :])
            else:
                out_ref[at, :] = value
            lse_ref[0, h : h + 1, at] = top + jnp.log(total)


def attend(qkv, slopes, lengths):
    _, slots, width = qkv.shape
    pairs = width // LANES

    def spec(i):
        return pl.BlockSpec((pl.Squeezed(), slots, LANES), lambda g, *_: (i, 0, g))

    return pl.pallas_call(
        attend_kernel,
        name="attend",
        out_shape=(
            jax.ShapeDtypeStruct((slots, width), BF16),
            jax.ShapeDtypeStruct((pairs, 2, slots), F32),
        ),
        grid_spec=pltpu.PrefetchScalarGridSpec(
            num_scalar_prefetch=2,
            grid=(pairs,),
            in_specs=[spec(0), spec(1), spec(2)],
            out_specs=(
                pl.BlockSpec((slots, LANES), lambda g, *_: (0, g)),
                pl.BlockSpec((1, 2, slots), lambda g, *_: (g, 0, 0)),
            ),
            scratch_shapes=[pltpu.VMEM((slots, TILE), F32), pltpu.VMEM((LANES, slots), BF16)],
        ),
        cost_estimate=pl.CostEstimate(flops=int(2e10), bytes_accessed=1 << 22, transcendentals=0),
        compiler_params=pltpu.CompilerParams(vmem_limit_bytes=VMEM_BYTES),
    )(lengths, slopes, qkv, qkv, qkv)


def unattend_kernel(
    len_ref, slope_ref, q_ref, k_ref, v_ref, do_ref, lse_ref, out_ref, bias, kt_v, dk_v, dv_v
):
    pair = pl.program_id(0)
    slots = q_ref.shape[0]
    lane = lax.broadcasted_iota(jnp.int32, (TILE, LANES), 1)
    causal = causal_tile()
    kt_v[...] = k_ref[...].T
    dk_v[...] = jnp.zeros_like(dk_v)
    dv_v[...] = jnp.zeros_like(dv_v)
    for h in range(2):
        mine = (lane >= HEAD_DIM) if h else (lane < HEAD_DIM)
        fill_bias(bias, slope_ref[pair * 2 + h], len_ref[0])
        for b in range(slots // TILE):
            at = slice(b * TILE, (b + 1) * TILE)
            query = jnp.where(mine, q_ref[at, :] * 0.125, 0).astype(BF16)
            grad = jnp.where(mine, do_ref[at, :], 0).astype(BF16)
            lse = lse_ref[0, h : h + 1, at]
            spans = [at] + ([slice(0, b * TILE)] if b else [])
            kept = []
            weighted = jnp.zeros((1, TILE), F32)
            for i, span in enumerate(spans):
                scores = dot_nt(k_ref[span, :], query) + bias[span, :]
                if i == 0:
                    scores = jnp.where(causal, scores, MASKED)
                probs = jnp.exp(scores - lse)
                d_probs = dot_nt(v_ref[span, :], grad)
                weighted += jnp.sum(probs * d_probs, axis=0, keepdims=True)
                kept.append((probs, d_probs))
                dv_v[span, :] += dot_nn(probs.astype(BF16), grad)
            d_query = jnp.zeros((LANES, TILE), F32)
            for span, (probs, d_probs) in zip(spans, kept):
                d_scores = (probs * (d_probs - weighted)).astype(BF16)
                dk_v[span, :] += dot_nn(d_scores, query)
                d_query += dot_nn(kt_v[:, span], d_scores)
            value = (d_query * 0.125).T.astype(BF16)
            if h:
                out_ref[0, at, :] = jnp.where(mine, value, out_ref[0, at, :])
            else:
                out_ref[0, at, :] = value
    out_ref[1, :, :] = dk_v[...].astype(BF16)
    out_ref[2, :, :] = dv_v[...].astype(BF16)


def unattend(qkv, d_attn, lse, slopes, lengths):
    _, slots, width = qkv.shape
    pairs = width // LANES

    def spec(i):
        return pl.BlockSpec((pl.Squeezed(), slots, LANES), lambda g, *_: (i, 0, g))

    return pl.pallas_call(
        unattend_kernel,
        name="unattend",
        out_shape=jax.ShapeDtypeStruct(qkv.shape, BF16),
        grid_spec=pltpu.PrefetchScalarGridSpec(
            num_scalar_prefetch=2,
            grid=(pairs,),
            in_specs=[
                spec(0),
                spec(1),
                spec(2),
                pl.BlockSpec((slots, LANES), lambda g, *_: (0, g)),
                pl.BlockSpec((1, 2, slots), lambda g, *_: (g, 0, 0)),
            ],
            out_specs=pl.BlockSpec((3, slots, LANES), lambda g, *_: (0, 0, g)),
            scratch_shapes=[
                pltpu.VMEM((slots, TILE), F32),
                pltpu.VMEM((LANES, slots), BF16),
                pltpu.VMEM((slots, LANES), F32),
                pltpu.VMEM((slots, LANES), F32),
            ],
        ),
        cost_estimate=pl.CostEstimate(flops=int(3e10), bytes_accessed=1 << 22, transcendentals=0),
        compiler_params=pltpu.CompilerParams(vmem_limit_bytes=VMEM_BYTES),
    )(lengths, slopes, qkv, qkv, qkv, d_attn, lse)


def norm_sum_kernel(nd, nt, x_ref, out_ref, from_t, total, from_d, t_send, t_recv, d_send, d_recv):
    d, t = lax.axis_index("dp"), lax.axis_index("tensor")
    barrier = pltpu.get_barrier_semaphore()
    for i in range(1, nt):
        peer = lax.rem(t + i, nt)
        pl.semaphore_signal(barrier, inc=1, device_id={"tensor": peer}, device_id_type=MESH)
    for i in range(1, nd):
        peer = lax.rem(d + i, nd)
        pl.semaphore_signal(barrier, inc=1, device_id={"dp": peer}, device_id_type=MESH)
    pl.semaphore_wait(barrier, nt + nd - 2)
    first = []
    for i in range(1, nt):
        peer = lax.rem(t + i, nt)
        first.append(
            pltpu.make_async_remote_copy(
                src_ref=x_ref.at[peer],
                dst_ref=from_t.at[i - 1],
                send_sem=t_send.at[i - 1],
                recv_sem=t_recv.at[i - 1],
                device_id={"tensor": peer},
                device_id_type=MESH,
            )
        )
    for copy in first:
        copy.start()
    total[...] = x_ref[t]
    for i, copy in enumerate(first):
        copy.wait_recv()
        total[...] += from_t[i]
    second = []
    for i in range(1, nd):
        peer = lax.rem(d + i, nd)
        second.append(
            pltpu.make_async_remote_copy(
                src_ref=total.at[peer],
                dst_ref=from_d.at[i - 1],
                send_sem=d_send.at[i - 1],
                recv_sem=d_recv.at[i - 1],
                device_id={"dp": peer},
                device_id_type=MESH,
            )
        )
    for copy in second:
        copy.start()
    out_ref[...] = total[d]
    for i, copy in enumerate(second):
        copy.wait_recv()
        out_ref[...] += from_d[i]
    for copy in first + second:
        copy.wait_send()


def norm_sum(local, nd, nt):
    lanes = local.shape[1] // (nd * nt)
    x = local.reshape(4, nd, nt, lanes).transpose(2, 1, 0, 3)
    x = jnp.pad(x, ((0, 0), (0, 0), (0, 4), (0, LANES - lanes)))
    vmem = pl.BlockSpec(memory_space=pltpu.VMEM)
    out = pl.pallas_call(
        functools.partial(norm_sum_kernel, nd, nt),
        name="norm_sum",
        out_shape=jax.ShapeDtypeStruct((8, LANES), F32),
        in_specs=[vmem],
        out_specs=vmem,
        scratch_shapes=[
            pltpu.VMEM((nt - 1, nd, 8, LANES), F32),
            pltpu.VMEM((nd, 8, LANES), F32),
            pltpu.VMEM((nd - 1, 8, LANES), F32),
            pltpu.SemaphoreType.DMA((nt - 1,)),
            pltpu.SemaphoreType.DMA((nt - 1,)),
            pltpu.SemaphoreType.DMA((nd - 1,)),
            pltpu.SemaphoreType.DMA((nd - 1,)),
        ],
        compiler_params=pltpu.CompilerParams(collective_id=6, has_side_effects=True),
    )(x)
    return out[:4, :lanes]


def per_device(tokens, w_qkv, w_out, w_up, w_down, norm_gains, norm_biases, lengths, cotangent):
    rows = tokens.shape[0]
    n, nd = lax.axis_size("tensor"), lax.axis_size("dp")
    norms = lax.all_gather(
        jnp.concatenate([norm_gains, norm_biases]).astype(BF16), "dp", axis=1, tiled=True
    ).astype(F32)
    gains, shifts = norms[:2], norms[2:]
    qkv_all = lax.all_gather(w_qkv.astype(BF16), "dp", axis=1, tiled=True)
    out_all = lax.all_gather(w_out.astype(BF16), "dp", axis=1, tiled=True)
    up_all = lax.all_gather(w_up.astype(BF16), "dp", axis=0, tiled=True)
    down_all = lax.all_gather(w_down.astype(BF16), "dp", axis=1, tiled=True)
    t = lax.axis_index("tensor")
    heads_local = qkv_all.shape[2] // HEAD_DIM
    head_ids = (t * heads_local + jnp.arange(heads_local, dtype=jnp.int32)).astype(F32)
    slopes = jnp.exp2(-8.0 * (head_ids + 1.0) / (heads_local * n))
    live_rows = (t * rows + jnp.arange(rows, dtype=jnp.int32) < lengths[0])[:, None]
    inputs = tokens.astype(F32)
    hat_one, inv_one = normalize(inputs)
    normed_one = (hat_one * gains[0] + shifts[0]).astype(BF16)
    qkv, normed_one_all = project(normed_one, qkv_all, n)
    attn, lse = attend(qkv, slopes, lengths)
    masked_cot = jnp.where(live_rows, cotangent, jnp.zeros_like(cotangent))
    attn_branch, masked_cot_all = branch(attn, out_all, masked_cot, n)
    after_attn = inputs + attn_branch
    hat_two, inv_two = normalize(after_attn)
    normed_two = (hat_two * gains[1] + shifts[1]).astype(BF16)
    normed_two_all, activated, d_up, mlp_part, d_norm_two = feed(
        normed_two, masked_cot_all, up_all, down_all, n
    )
    gain_two = jnp.sum(d_norm_two * hat_two, axis=0)
    shift_two = jnp.sum(d_norm_two, axis=0)
    d_after = masked_cot.astype(F32) + norm_back(d_norm_two, hat_two, inv_two, gains[1])
    d_branch = d_after.astype(BF16)
    grad_down = dot_tn(activated, masked_cot_all).astype(BF16)
    down_shard = lax.psum_scatter(grad_down, "dp", scatter_dimension=1, tiled=True).astype(F32)
    grad_up = dot_tn(normed_two_all, d_up).astype(BF16)
    up_shard = lax.psum_scatter(grad_up, "dp", scatter_dimension=0, tiled=True).astype(F32)
    d_branch_all, d_attn, mlp_branch = unbranch(d_branch, out_all, mlp_part, n)
    output = jnp.where(live_rows, after_attn + mlp_branch, 0.0).astype(BF16)
    grad_out = dot_tn(attn, d_branch_all).astype(BF16)
    out_shard = lax.psum_scatter(grad_out, "dp", scatter_dimension=1, tiled=True).astype(F32)
    d_qkv = unattend(qkv, d_attn, lse, slopes, lengths)
    grad_qkv = jnp.stack([dot_tn(normed_one_all, d_qkv[i]) for i in range(3)]).astype(BF16)
    qkv_shard = lax.psum_scatter(grad_qkv, "dp", scatter_dimension=1, tiled=True).astype(F32)
    d_norm_one = unproject(d_qkv, qkv_all, rows, n)
    gain_one = jnp.sum(d_norm_one * hat_one, axis=0)
    shift_one = jnp.sum(d_norm_one, axis=0)
    input_grad = (d_after + norm_back(d_norm_one, hat_one, inv_one, gains[0])).astype(BF16)
    sums = norm_sum(jnp.stack([gain_one, gain_two, shift_one, shift_two]), nd, n)
    return (output, input_grad, qkv_shard, out_shard, up_shard, down_shard, sums[:2], sums[2:])


def solution(mesh):
    placed = (
        P(("dp", "tensor"), None),
        P(None, "dp", "tensor"),
        P("tensor", "dp"),
        P("dp", "tensor"),
        P("tensor", "dp"),
        P(None, "dp"),
        P(None, "dp"),
        P("dp"),
        P(("dp", "tensor"), None),
    )
    return jax.shard_map(
        per_device,
        mesh=mesh,
        in_specs=placed,
        out_specs=(
            P(("dp", "tensor"), None),
            P(("dp", "tensor"), None),
            P(None, "dp", "tensor"),
            P("tensor", "dp"),
            P("dp", "tensor"),
            P("tensor", "dp"),
            P(None, ("dp", "tensor")),
            P(None, ("dp", "tensor")),
        ),
        check_vma=False,
    )
```

```python
import functools

import jax
import jax.numpy as jnp
from jax import lax
from jax.experimental import pallas as pl
from jax.experimental.pallas import tpu as pltpu
from jax.sharding import PartitionSpec as P

HEAD_DIM = 64
LANES = 128
TILE = 256
PARTS = 4
CHUNK = 64
VMEM_BYTES = 60 * 1024 * 1024

EPSILON = 1e-05
MASKED = -1e30
INV_ROOT_TAU = 0.3989422804014327
ROOT_HALF = 0.7071067811865476

MESH = pl.DeviceIdType.MESH
ANY = pl.BlockSpec(memory_space=pl.ANY)
F32 = jnp.float32
BF16 = jnp.bfloat16


def dot_nn(left, right):
    return lax.dot_general(left, right, (((1,), (0,)), ((), ())), preferred_element_type=F32)


def dot_nt(left, right):
    return lax.dot_general(left, right, (((1,), (1,)), ((), ())), preferred_element_type=F32)


def dot_tn(left, right):
    return lax.dot_general(left, right, (((0,), (0,)), ((), ())), preferred_element_type=F32)


def normalize(values):
    center = jnp.mean(values, axis=-1, keepdims=True)
    offset = values - center
    spread = jnp.mean(offset * offset, axis=-1, keepdims=True)
    inv_std = lax.rsqrt(spread + EPSILON)
    return (offset * inv_std, inv_std)


def norm_back(grads, normed, inv_std, gain):
    scaled = grads * gain
    return inv_std * (
        scaled
        - jnp.mean(scaled, axis=-1, keepdims=True)
        - normed * jnp.mean(scaled * normed, axis=-1, keepdims=True)
    )


def block_at(index, size):
    return pl.ds(pl.multiple_of(index * size, size), size)


def line_enter(p, n, more=0):
    barrier = pltpu.get_barrier_semaphore()

    @pl.when(p > 0)
    def _():
        pl.semaphore_signal(barrier, inc=1, device_id={"tensor": p - 1}, device_id_type=MESH)

    @pl.when(p < n - 1)
    def _():
        pl.semaphore_signal(barrier, inc=1, device_id={"tensor": p + 1}, device_id_type=MESH)

    pl.semaphore_wait(barrier, jnp.where(p > 0, 1, 0) + jnp.where(p < n - 1, 1, 0) + more)


class Line:
    def __init__(self, n, rows):
        self.n = n
        self.p = lax.axis_index("tensor")
        self.rows = rows
        self.piece = rows // PARTS
        self.right = lax.rem(self.p + 1, n)
        self.left = lax.rem(self.p + n - 1, n)

    def slot(self, ref, j, c):
        start = pl.multiple_of(j * self.rows + c * self.piece, self.piece)
        return ref.at[pl.ds(start, self.piece)]

    def shard(self, ref, j):
        return ref.at[block_at(j, self.rows)]


class Gather:
    def __init__(self, line, buf, right_sem, left_sem, recv_sem):
        self.line, self.buf = line, buf
        self.right_sem, self.left_sem, self.recv_sem = right_sem, left_sem, recv_sem

    def copy(self, j, c, rightward):
        line = self.line
        slot = line.slot(self.buf, j, c)
        i = j * PARTS + c
        return pltpu.make_async_remote_copy(
            src_ref=slot,
            dst_ref=slot,
            send_sem=(self.right_sem if rightward else self.left_sem).at[i],
            recv_sem=self.recv_sem.at[i],
            device_id={"tensor": line.right if rightward else line.left},
            device_id_type=MESH,
        )

    def begin(self):
        p, n = self.line.p, self.line.n
        for c in range(PARTS):

            @pl.when(p < n - 1)
            def _():
                self.copy(p, c, True).start()

            @pl.when(p > 0)
            def _():
                self.copy(p, c, False).start()

    def step(self, s, c):
        p, n = self.line.p, self.line.n

        @pl.when(p - s >= 0)
        def _():
            copy = self.copy(p - s, c, True)
            copy.wait_recv()

            @pl.when(p < n - 1)
            def _():
                copy.start()

        @pl.when(p + s < n)
        def _():
            copy = self.copy(p + s, c, False)
            copy.wait_recv()

            @pl.when(p > 0)
            def _():
                copy.start()

    def end(self):
        p, n = self.line.p, self.line.n

        @pl.loop(0, n)
        def _(j):
            for c in range(PARTS):

                @pl.when((j <= p) & (p < n - 1))
                def _():
                    self.copy(j, c, True).wait_send()

                @pl.when((j >= p) & (p > 0))
                def _():
                    self.copy(j, c, False).wait_send()


class Scatter:
    def __init__(self, line, part, from_left, from_right, right_sem, left_sem, lrecv_sem, rrecv_sem):
        self.line, self.part, self.from_left, self.from_right = line, part, from_left, from_right
        self.right_sem, self.left_sem = right_sem, left_sem
        self.lrecv_sem, self.rrecv_sem = lrecv_sem, rrecv_sem

    def copy(self, j, c, rightward):
        line = self.line
        i = j * PARTS + c
        return pltpu.make_async_remote_copy(
            src_ref=line.slot(self.part, j, c),
            dst_ref=line.slot(self.from_left if rightward else self.from_right, j, c),
            send_sem=(self.right_sem if rightward else self.left_sem).at[i],
            recv_sem=(self.lrecv_sem if rightward else self.rrecv_sem).at[i],
            device_id={"tensor": line.right if rightward else line.left},
            device_id_type=MESH,
        )

    def add(self, j, c, ref):
        part = self.line.slot(self.part, j, c)
        total = part[...].astype(F32) + self.line.slot(ref, j, c)[...].astype(F32)
        part[...] = total.astype(BF16)

    def send_right(self, j, c):
        p, n = self.line.p, self.line.n

        @pl.when((j > p) & (j < n))
        def _():
            copy = self.copy(j, c, True)

            @pl.when(p > 0)
            def _():
                copy.wait_recv()
                self.add(j, c, self.from_left)

            copy.start()

    def send_left(self, j, c):
        p, n = self.line.p, self.line.n

        @pl.when((j < p) & (j >= 0))
        def _():
            copy = self.copy(j, c, False)

            @pl.when(p < n - 1)
            def _():
                copy.wait_recv()
                self.add(j, c, self.from_right)

            copy.start()

    def finish(self, out):
        p, n = self.line.p, self.line.n
        piece = self.line.piece
        for c in range(PARTS):
            mine = out.at[pl.ds(c * piece, piece)]
            mine[...] = self.line.slot(self.part, p, c)[...].astype(F32)

            @pl.when(p > 0)
            def _():
                self.copy(p, c, True).wait_recv()
                mine[...] += self.line.slot(self.from_left, p, c)[...].astype(F32)

            @pl.when(p < n - 1)
            def _():
                self.copy(p, c, False).wait_recv()
                mine[...] += self.line.slot(self.from_right, p, c)[...].astype(F32)

    def end(self):
        p, n = self.line.p, self.line.n

        @pl.loop(0, n)
        def _(j):
            for c in range(PARTS):

                @pl.when(j > p)
                def _():
                    self.copy(j, c, True).wait_send()

                @pl.when(j < p)
                def _():
                    self.copy(j, c, False).wait_send()


def line_sems(n):
    return pltpu.SemaphoreType.DMA((n * PARTS,))


def remote_call(body, name, collective_id, outs, scratch, micros, *args):
    return pl.pallas_call(
        body,
        name=name,
        out_shape=outs,
        in_specs=[ANY] * len(args),
        out_specs=jax.tree.map(lambda _: ANY, outs),
        scratch_shapes=scratch,
        cost_estimate=pl.CostEstimate(
            flops=int(micros * 1e-6 * 1.15e15), bytes_accessed=1 << 20, transcendentals=0
        ),
        compiler_params=pltpu.CompilerParams(
            collective_id=collective_id, has_side_effects=True, vmem_limit_bytes=VMEM_BYTES
        ),
    )(*args)


def gather_kernel(
    n, nd, rows, x_ref, nrm_ref, h_ref, norms_ref,
    buf, h_v, nrm_v, all_v, right_sem, left_sem, recv_sem, nsend_sem, nrecv_sem, load_sem, store_sem,
):
    line = Line(n, rows)
    p = line.p
    d = lax.axis_index("dp")
    load_x = pltpu.make_async_copy(x_ref, line.shard(buf, p), load_sem.at[0])
    load_n = pltpu.make_async_copy(nrm_ref, nrm_v.at[d], load_sem.at[1])
    load_x.start()
    load_n.start()
    barrier = pltpu.get_barrier_semaphore()
    for i in range(1, nd):
        peer = lax.rem(d + i, nd)
        pl.semaphore_signal(barrier, inc=1, device_id={"dp": peer}, device_id_type=MESH)
    line_enter(p, n, nd - 1)
    load_x.wait()
    gather = Gather(line, buf, right_sem, left_sem, recv_sem)
    gather.begin()
    load_n.wait()

    def norm_copy(i, source):
        return pltpu.make_async_remote_copy(
            src_ref=nrm_v.at[source],
            dst_ref=nrm_v.at[source],
            send_sem=nsend_sem.at[i],
            recv_sem=nrecv_sem.at[i],
            device_id={"dp": lax.rem(d + i, nd)},
            device_id_type=MESH,
        )

    for i in range(1, nd):
        norm_copy(i, d).start()
    for i in range(1, nd):
        norm_copy(i, lax.rem(d + nd - i, nd)).wait_recv()
    all_v[...] = jnp.concatenate([nrm_v[i] for i in range(nd)], axis=1)
    store_n = pltpu.make_async_copy(all_v, norms_ref, load_sem.at[0])
    store_n.start()

    def store(j):
        at = block_at(j, rows)
        return pltpu.make_async_copy(h_v.at[at], h_ref.at[at], store_sem.at[j])

    def compute(j):
        @pl.loop(0, rows // CHUNK)
        def _(i):
            at = pl.ds(pl.multiple_of(j * rows + i * CHUNK, CHUNK), CHUNK)
            hat, _ = normalize(buf[at, :].astype(F32))
            h_v[at, :] = (hat * all_v[0:1, :] + all_v[2:3, :]).astype(BF16)

        store(j).start()

    compute(p)

    @pl.loop(1, n)
    def _(s):
        for c in range(PARTS):
            gather.step(s, c)

        @pl.when(p - s >= 0)
        def _():
            compute(p - s)

        @pl.when(p + s < n)
        def _():
            compute(p + s)

    gather.end()
    store_n.wait()
    for i in range(1, nd):
        norm_copy(i, d).wait_send()

    @pl.loop(0, n)
    def _(j):
        store(j).wait()


def gather_rows(tokens, local_norms, n, nd):
    rows, model = tokens.shape
    group = n * rows
    return remote_call(
        functools.partial(gather_kernel, n, nd, rows),
        "gather_rows",
        1,
        (jax.ShapeDtypeStruct((group, model), BF16), jax.ShapeDtypeStruct((8, model), F32)),
        [
            pltpu.VMEM((group, model), BF16),
            pltpu.VMEM((group, model), BF16),
            pltpu.VMEM((nd, 8, model // nd), F32),
            pltpu.VMEM((8, model), F32),
            line_sems(n),
            line_sems(n),
            line_sems(n),
            pltpu.SemaphoreType.DMA((nd,)),
            pltpu.SemaphoreType.DMA((nd,)),
            pltpu.SemaphoreType.DMA((2,)),
            pltpu.SemaphoreType.DMA((n,)),
        ],
        75,
        tokens,
        local_norms,
    )


def project_kernel(h_ref, w_ref, out_ref):
    out_ref[...] = dot_nn(h_ref[...], w_ref[...]).astype(BF16)


def project(normed, weights):
    group, model = normed.shape
    width = weights.shape[2]
    return pl.pallas_call(
        project_kernel,
        name="project",
        out_shape=jax.ShapeDtypeStruct((3, group, width), BF16),
        grid=(3, width // TILE),
        in_specs=[
            pl.BlockSpec((group, model), lambda i, t: (0, 0)),
            pl.BlockSpec((pl.Squeezed(), model, TILE), lambda i, t: (i, 0, t)),
        ],
        out_specs=pl.BlockSpec((pl.Squeezed(), group, TILE), lambda i, t: (i, 0, t)),
        cost_estimate=pl.CostEstimate(flops=int(1e10), bytes_accessed=1 << 23, transcendentals=0),
        compiler_params=pltpu.CompilerParams(vmem_limit_bytes=VMEM_BYTES),
    )(normed, weights)


def branch_kernel(
    n, rows, attn_ref, w_ref, g_ref, out_ref, all_ref,
    a_v, w_v, buf, part, from_left, from_right, out_v,
    gr_sem, gl_sem, grecv_sem, sr_sem, sl_sem, lrecv_sem, rrecv_sem, load_sem, store_sem,
):
    line = Line(n, rows)
    p = line.p
    model = w_v.shape[1]
    loads = (
        pltpu.make_async_copy(g_ref, line.shard(buf, p), load_sem.at[0]),
        pltpu.make_async_copy(attn_ref, a_v, load_sem.at[1]),
        pltpu.make_async_copy(w_ref, w_v, load_sem.at[2]),
    )
    for copy in loads:
        copy.start()
    line_enter(p, n)
    for copy in loads:
        copy.wait()
    gather = Gather(line, buf, gr_sem, gl_sem, grecv_sem)
    scatter = Scatter(line, part, from_left, from_right, sr_sem, sl_sem, lrecv_sem, rrecv_sem)
    gather.begin()

    def compute(j):
        at = block_at(j, rows)

        @pl.loop(0, model // TILE)
        def _(t):
            cols = block_at(t, TILE)
            part[at, cols] = dot_nn(a_v[at, :], w_v[:, cols]).astype(BF16)

    @pl.loop(0, n)
    def _(s):
        right, left = n - 1 - s, s

        @pl.when(right > p)
        def _():
            compute(right)

        @pl.when(left < p)
        def _():
            compute(left)

        for c in range(PARTS):
            scatter.send_right(right, c)
            scatter.send_left(left, c)

            @pl.when(s + 1 < n)
            def _():
                gather.step(s + 1, c)

    compute(p)
    scatter.finish(out_v)
    stores = (
        pltpu.make_async_copy(out_v, out_ref, store_sem.at[0]),
        pltpu.make_async_copy(buf, all_ref, store_sem.at[1]),
    )
    for copy in stores:
        copy.start()
    scatter.end()
    gather.end()
    for copy in stores:
        copy.wait()


def branch(attn, w_out, cot, n):
    rows, model = cot.shape
    group = n * rows
    full = pltpu.VMEM((group, model), BF16)
    return remote_call(
        functools.partial(branch_kernel, n, rows),
        "branch",
        2,
        (jax.ShapeDtypeStruct((rows, model), F32), jax.ShapeDtypeStruct((group, model), BF16)),
        [
            pltpu.VMEM(attn.shape, BF16),
            pltpu.VMEM(w_out.shape, BF16),
            full, full, full, full,
            pltpu.VMEM((rows, model), F32),
        ]
        + [line_sems(n)] * 7
        + [pltpu.SemaphoreType.DMA((3,)), pltpu.SemaphoreType.DMA((2,))],
        100,
        attn,
        w_out,
        cot,
    )


def feed_kernel(
    n, rows, h_ref, g_ref, up_ref, down_ref, all_ref, act_ref, dup_ref, mlp_ref, dh_ref,
    buf, up_v, down_v, g_v, act_v, dup_v, mlp_v, part, from_left, from_right, out_v,
    gr_sem, gl_sem, grecv_sem, sr_sem, sl_sem, lrecv_sem, rrecv_sem, load_sem, store_sem,
):
    line = Line(n, rows)
    p = line.p
    model, hidden = up_v.shape
    load_h = pltpu.make_async_copy(h_ref, line.shard(buf, p), load_sem.at[0])
    loads = (
        pltpu.make_async_copy(up_ref, up_v, load_sem.at[1]),
        pltpu.make_async_copy(g_ref, g_v, load_sem.at[2]),
        pltpu.make_async_copy(down_ref, down_v, load_sem.at[3]),
    )
    load_h.start()
    for copy in loads:
        copy.start()
    line_enter(p, n)
    load_h.wait()
    gather = Gather(line, buf, gr_sem, gl_sem, grecv_sem)
    scatter = Scatter(line, part, from_left, from_right, sr_sem, sl_sem, lrecv_sem, rrecv_sem)
    gather.begin()
    for copy in loads:
        copy.wait()

    def stores(j):
        at = block_at(j, rows)
        return (
            pltpu.make_async_copy(buf.at[at], all_ref.at[at], store_sem.at[0, j]),
            pltpu.make_async_copy(act_v.at[at], act_ref.at[at], store_sem.at[1, j]),
            pltpu.make_async_copy(dup_v.at[at], dup_ref.at[at], store_sem.at[2, j]),
            pltpu.make_async_copy(mlp_v.at[at], mlp_ref.at[at], store_sem.at[3, j]),
        )

    def compute(j):
        at = block_at(j, rows)

        @pl.loop(0, hidden // TILE)
        def _(t):
            cols = block_at(t, TILE)
            up = dot_nn(buf[at, :], up_v[:, cols])
            d_act = dot_nt(g_v[at, :], down_v[cols, :])
            half = 0.5 * (1.0 + lax.erf(up * ROOT_HALF))
            act_v[at, cols] = (up * half).astype(BF16)
            slope = half + up * jnp.exp(-0.5 * up * up) * INV_ROOT_TAU
            dup_v[at, cols] = (d_act * slope).astype(BF16)

        @pl.loop(0, model // TILE)
        def _(t):
            cols = block_at(t, TILE)
            part[at, cols] = dot_nt(dup_v[at, :], up_v[cols, :]).astype(BF16)

    def compute_down(j):
        at = block_at(j, rows)

        @pl.loop(0, model // TILE)
        def _(t):
            cols = block_at(t, TILE)
            mlp_v[at, cols] = dot_nn(act_v[at, :], down_v[:, cols]).astype(BF16)

        for copy in stores(j):
            copy.start()

    compute(p)
    compute_down(p)

    @pl.loop(1, n)
    def _(s):
        for c in range(PARTS):
            gather.step(s, c)

        @pl.when(p - s >= 0)
        def _():
            compute(p - s)

            @pl.when(p == n - 1)
            def _():
                for c in range(PARTS):
                    scatter.send_left(p - s, c)

            compute_down(p - s)

        @pl.when(p + s < n)
        def _():
            compute(p + s)

            @pl.when(p == 0)
            def _():
                for c in range(PARTS):
                    scatter.send_right(p + s, c)

            compute_down(p + s)

    @pl.loop(1, 2 * n - 2)
    def _(s):
        for c in range(PARTS):

            @pl.when(p > 0)
            def _():
                scatter.send_right(s - p, c)

            @pl.when(p < n - 1)
            def _():
                scatter.send_left(2 * (n - 1) - p - s, c)

    scatter.finish(out_v)
    store_out = pltpu.make_async_copy(out_v, dh_ref, load_sem.at[0])
    store_out.start()
    scatter.end()
    gather.end()

    @pl.loop(0, n)
    def _(j):
        for copy in stores(j):
            copy.wait()

    store_out.wait()


def feed(normed, cot_all, w_up, w_down, n):
    rows, model = normed.shape
    hidden = w_up.shape[1]
    group = n * rows
    full = pltpu.VMEM((group, model), BF16)
    wide = pltpu.VMEM((group, hidden), BF16)
    return remote_call(
        functools.partial(feed_kernel, n, rows),
        "feed",
        3,
        (
            jax.ShapeDtypeStruct((group, model), BF16),
            jax.ShapeDtypeStruct((group, hidden), BF16),
            jax.ShapeDtypeStruct((group, hidden), BF16),
            jax.ShapeDtypeStruct((group, model), BF16),
            jax.ShapeDtypeStruct((rows, model), F32),
        ),
        [
            full,
            pltpu.VMEM(w_up.shape, BF16),
            pltpu.VMEM(w_down.shape, BF16),
            full,
            wide,
            wide,
            full, full, full, full,
            pltpu.VMEM((rows, model), F32),
        ]
        + [line_sems(n)] * 7
        + [pltpu.SemaphoreType.DMA((4,)), pltpu.SemaphoreType.DMA((4, n))],
        140,
        normed,
        cot_all,
        w_up,
        w_down,
    )


def unbranch_kernel(
    n, rows, d_ref, w_ref, mlp_ref, all_ref, da_ref, out_ref,
    buf, w_v, a_v, part, from_left, from_right, out_v,
    gr_sem, gl_sem, grecv_sem, sr_sem, sl_sem, lrecv_sem, rrecv_sem, load_sem, store_sem,
):
    line = Line(n, rows)
    p = line.p
    width, model = w_v.shape
    loads = (
        pltpu.make_async_copy(d_ref, line.shard(buf, p), load_sem.at[0]),
        pltpu.make_async_copy(mlp_ref, part, load_sem.at[1]),
        pltpu.make_async_copy(w_ref, w_v, load_sem.at[2]),
    )
    for copy in loads:
        copy.start()
    line_enter(p, n)
    for copy in loads:
        copy.wait()
    gather = Gather(line, buf, gr_sem, gl_sem, grecv_sem)
    scatter = Scatter(line, part, from_left, from_right, sr_sem, sl_sem, lrecv_sem, rrecv_sem)
    gather.begin()

    def compute(j):
        at = block_at(j, rows)

        @pl.loop(0, width // TILE)
        def _(t):
            cols = block_at(t, TILE)
            a_v[at, cols] = dot_nt(buf[at, :], w_v[cols, :]).astype(BF16)

    @pl.loop(0, n)
    def _(s):
        for c in range(PARTS):

            @pl.when(s > 0)
            def _():
                gather.step(s, c)

            scatter.send_right(n - 1 - s, c)
            scatter.send_left(s, c)

        @pl.when(p - s >= 0)
        def _():
            compute(p - s)

        @pl.when((p + s < n) & (s > 0))
        def _():
            compute(p + s)

    scatter.finish(out_v)
    stores = (
        pltpu.make_async_copy(out_v, out_ref, store_sem.at[0]),
        pltpu.make_async_copy(buf, all_ref, store_sem.at[1]),
        pltpu.make_async_copy(a_v, da_ref, store_sem.at[2]),
    )
    for copy in stores:
        copy.start()
    scatter.end()
    gather.end()
    for copy in stores:
        copy.wait()


def unbranch(d_branch, w_out, mlp_part, n):
    rows, model = d_branch.shape
    group = n * rows
    width = w_out.shape[0]
    full = pltpu.VMEM((group, model), BF16)
    return remote_call(
        functools.partial(unbranch_kernel, n, rows),
        "unbranch",
        4,
        (
            jax.ShapeDtypeStruct((group, model), BF16),
            jax.ShapeDtypeStruct((group, width), BF16),
            jax.ShapeDtypeStruct((rows, model), F32),
        ),
        [
            full,
            pltpu.VMEM(w_out.shape, BF16),
            pltpu.VMEM((group, width), BF16),
            full, full, full,
            pltpu.VMEM((rows, model), F32),
        ]
        + [line_sems(n)] * 7
        + [pltpu.SemaphoreType.DMA((3,)), pltpu.SemaphoreType.DMA((3,))],
        100,
        d_branch,
        w_out,
        mlp_part,
    )


def unproject_kernel(
    n, rows, d_ref, w_ref, out_ref,
    d_v, w_v, part, from_left, from_right, out_v,
    sr_sem, sl_sem, lrecv_sem, rrecv_sem, load_sem,
):
    line = Line(n, rows)
    p = line.p
    model = w_v.shape[1]
    loads = (
        pltpu.make_async_copy(d_ref, d_v, load_sem.at[0]),
        pltpu.make_async_copy(w_ref, w_v, load_sem.at[1]),
    )
    for copy in loads:
        copy.start()
    line_enter(p, n)
    for copy in loads:
        copy.wait()
    scatter = Scatter(line, part, from_left, from_right, sr_sem, sl_sem, lrecv_sem, rrecv_sem)

    def compute(j):
        at = block_at(j, rows)

        @pl.loop(0, model // TILE)
        def _(t):
            cols = block_at(t, TILE)
            total = dot_nt(d_v[0, at, :], w_v[0, cols, :])
            total += dot_nt(d_v[1, at, :], w_v[1, cols, :])
            total += dot_nt(d_v[2, at, :], w_v[2, cols, :])
            part[at, cols] = total.astype(BF16)

    @pl.loop(0, n)
    def _(s):
        right, left = n - 1 - s, s

        @pl.when(right > p)
        def _():
            compute(right)

        @pl.when(left < p)
        def _():
            compute(left)

        for c in range(PARTS):
            scatter.send_right(right, c)
            scatter.send_left(left, c)

    compute(p)
    scatter.finish(out_v)
    store = pltpu.make_async_copy(out_v, out_ref, load_sem.at[0])
    store.start()
    scatter.end()
    store.wait()


def unproject(d_qkv, weights, rows, n):
    model = weights.shape[1]
    group = n * rows
    full = pltpu.VMEM((group, model), BF16)
    return remote_call(
        functools.partial(unproject_kernel, n, rows),
        "unproject",
        5,
        jax.ShapeDtypeStruct((rows, model), F32),
        [
            pltpu.VMEM(d_qkv.shape, BF16),
            pltpu.VMEM(weights.shape, BF16),
            full, full, full,
            pltpu.VMEM((rows, model), F32),
        ]
        + [line_sems(n)] * 4
        + [pltpu.SemaphoreType.DMA((2,))],
        80,
        d_qkv,
        weights,
    )


def fill_bias(bias, slope, length):
    row = lax.broadcasted_iota(jnp.int32, bias.shape, 0)
    bias[...] = jnp.where(row < length, slope * row.astype(F32), MASKED)


def causal_tile():
    shape = (TILE, TILE)
    return lax.broadcasted_iota(jnp.int32, shape, 0) <= lax.broadcasted_iota(jnp.int32, shape, 1)


def attend_kernel(len_ref, slope_ref, q_ref, k_ref, v_ref, out_ref, lse_ref, bias, vt_v):
    pair = pl.program_id(0)
    slots = q_ref.shape[0]
    lane = lax.broadcasted_iota(jnp.int32, (TILE, LANES), 1)
    causal = causal_tile()
    vt_v[...] = v_ref[...].T
    for h in range(2):
        mine = (lane >= HEAD_DIM) if h else (lane < HEAD_DIM)
        fill_bias(bias, slope_ref[pair * 2 + h], len_ref[0])
        for b in range(slots // TILE):
            at = slice(b * TILE, (b + 1) * TILE)
            end = (b + 1) * TILE
            query = jnp.where(mine, q_ref[at, :] * 0.125, 0).astype(BF16)
            last = dot_nt(k_ref[at, :], query) + bias[at, :]
            last = jnp.where(causal, last, MASKED)
            top = jnp.max(last, axis=0, keepdims=True)
            if b > 0:
                first = dot_nt(k_ref[: b * TILE, :], query) + bias[: b * TILE, :]
                top = jnp.maximum(top, jnp.max(first, axis=0, keepdims=True))
            probs = jnp.exp(last - top)
            total = jnp.sum(probs, axis=0, keepdims=True)
            mixed = dot_nn(vt_v[:, at], probs.astype(BF16))
            if b > 0:
                probs = jnp.exp(first - top)
                total += jnp.sum(probs, axis=0, keepdims=True)
                mixed += dot_nn(vt_v[:, : b * TILE], probs.astype(BF16))
            value = (mixed / total).T.astype(BF16)
            if h:
                out_ref[at, :] = jnp.where(mine, value, out_ref[at, :])
            else:
                out_ref[at, :] = value
            lse_ref[0, h : h + 1, at] = top + jnp.log(total)


def attend(qkv, slopes, lengths):
    _, slots, width = qkv.shape
    pairs = width // LANES

    def spec(i):
        return pl.BlockSpec((pl.Squeezed(), slots, LANES), lambda g, *_: (i, 0, g))

    return pl.pallas_call(
        attend_kernel,
        name="attend",
        out_shape=(
            jax.ShapeDtypeStruct((slots, width), BF16),
            jax.ShapeDtypeStruct((pairs, 2, slots), F32),
        ),
        grid_spec=pltpu.PrefetchScalarGridSpec(
            num_scalar_prefetch=2,
            grid=(pairs,),
            in_specs=[spec(0), spec(1), spec(2)],
            out_specs=(
                pl.BlockSpec((slots, LANES), lambda g, *_: (0, g)),
                pl.BlockSpec((1, 2, slots), lambda g, *_: (g, 0, 0)),
            ),
            scratch_shapes=[pltpu.VMEM((slots, TILE), F32), pltpu.VMEM((LANES, slots), BF16)],
        ),
        cost_estimate=pl.CostEstimate(flops=int(2e10), bytes_accessed=1 << 22, transcendentals=0),
        compiler_params=pltpu.CompilerParams(vmem_limit_bytes=VMEM_BYTES),
    )(lengths, slopes, qkv, qkv, qkv)


def unattend_kernel(
    len_ref, slope_ref, q_ref, k_ref, v_ref, do_ref, lse_ref, out_ref, bias, kt_v, dk_v, dv_v
):
    pair = pl.program_id(0)
    slots = q_ref.shape[0]
    lane = lax.broadcasted_iota(jnp.int32, (TILE, LANES), 1)
    causal = causal_tile()
    kt_v[...] = k_ref[...].T
    dk_v[...] = jnp.zeros_like(dk_v)
    dv_v[...] = jnp.zeros_like(dv_v)
    for h in range(2):
        mine = (lane >= HEAD_DIM) if h else (lane < HEAD_DIM)
        fill_bias(bias, slope_ref[pair * 2 + h], len_ref[0])
        for b in range(slots // TILE):
            at = slice(b * TILE, (b + 1) * TILE)
            query = jnp.where(mine, q_ref[at, :] * 0.125, 0).astype(BF16)
            grad = jnp.where(mine, do_ref[at, :], 0).astype(BF16)
            lse = lse_ref[0, h : h + 1, at]
            spans = [at] + ([slice(0, b * TILE)] if b else [])
            kept = []
            weighted = jnp.zeros((1, TILE), F32)
            for i, span in enumerate(spans):
                scores = dot_nt(k_ref[span, :], query) + bias[span, :]
                if i == 0:
                    scores = jnp.where(causal, scores, MASKED)
                probs = jnp.exp(scores - lse)
                d_probs = dot_nt(v_ref[span, :], grad)
                weighted += jnp.sum(probs * d_probs, axis=0, keepdims=True)
                kept.append((probs, d_probs))
                dv_v[span, :] += dot_nn(probs.astype(BF16), grad)
            d_query = jnp.zeros((LANES, TILE), F32)
            for span, (probs, d_probs) in zip(spans, kept):
                d_scores = (probs * (d_probs - weighted)).astype(BF16)
                dk_v[span, :] += dot_nn(d_scores, query)
                d_query += dot_nn(kt_v[:, span], d_scores)
            value = (d_query * 0.125).T.astype(BF16)
            if h:
                out_ref[0, at, :] = jnp.where(mine, value, out_ref[0, at, :])
            else:
                out_ref[0, at, :] = value
    out_ref[1, :, :] = dk_v[...].astype(BF16)
    out_ref[2, :, :] = dv_v[...].astype(BF16)


def unattend(qkv, d_attn, lse, slopes, lengths):
    _, slots, width = qkv.shape
    pairs = width // LANES

    def spec(i):
        return pl.BlockSpec((pl.Squeezed(), slots, LANES), lambda g, *_: (i, 0, g))

    return pl.pallas_call(
        unattend_kernel,
        name="unattend",
        out_shape=jax.ShapeDtypeStruct(qkv.shape, BF16),
        grid_spec=pltpu.PrefetchScalarGridSpec(
            num_scalar_prefetch=2,
            grid=(pairs,),
            in_specs=[
                spec(0),
                spec(1),
                spec(2),
                pl.BlockSpec((slots, LANES), lambda g, *_: (0, g)),
                pl.BlockSpec((1, 2, slots), lambda g, *_: (g, 0, 0)),
            ],
            out_specs=pl.BlockSpec((3, slots, LANES), lambda g, *_: (0, 0, g)),
            scratch_shapes=[
                pltpu.VMEM((slots, TILE), F32),
                pltpu.VMEM((LANES, slots), BF16),
                pltpu.VMEM((slots, LANES), F32),
                pltpu.VMEM((slots, LANES), F32),
            ],
        ),
        cost_estimate=pl.CostEstimate(flops=int(3e10), bytes_accessed=1 << 22, transcendentals=0),
        compiler_params=pltpu.CompilerParams(vmem_limit_bytes=VMEM_BYTES),
    )(lengths, slopes, qkv, qkv, qkv, d_attn, lse)


def norm_sum_kernel(nd, nt, x_ref, out_ref, from_t, total, from_d, t_send, t_recv, d_send, d_recv):
    d, t = lax.axis_index("dp"), lax.axis_index("tensor")
    barrier = pltpu.get_barrier_semaphore()
    for i in range(1, nt):
        peer = lax.rem(t + i, nt)
        pl.semaphore_signal(barrier, inc=1, device_id={"tensor": peer}, device_id_type=MESH)
    for i in range(1, nd):
        peer = lax.rem(d + i, nd)
        pl.semaphore_signal(barrier, inc=1, device_id={"dp": peer}, device_id_type=MESH)
    pl.semaphore_wait(barrier, nt + nd - 2)
    first = []
    for i in range(1, nt):
        peer = lax.rem(t + i, nt)
        first.append(
            pltpu.make_async_remote_copy(
                src_ref=x_ref.at[peer],
                dst_ref=from_t.at[i - 1],
                send_sem=t_send.at[i - 1],
                recv_sem=t_recv.at[i - 1],
                device_id={"tensor": peer},
                device_id_type=MESH,
            )
        )
    for copy in first:
        copy.start()
    total[...] = x_ref[t]
    for i, copy in enumerate(first):
        copy.wait_recv()
        total[...] += from_t[i]
    second = []
    for i in range(1, nd):
        peer = lax.rem(d + i, nd)
        second.append(
            pltpu.make_async_remote_copy(
                src_ref=total.at[peer],
                dst_ref=from_d.at[i - 1],
                send_sem=d_send.at[i - 1],
                recv_sem=d_recv.at[i - 1],
                device_id={"dp": peer},
                device_id_type=MESH,
            )
        )
    for copy in second:
        copy.start()
    out_ref[...] = total[d]
    for i, copy in enumerate(second):
        copy.wait_recv()
        out_ref[...] += from_d[i]
    for copy in first + second:
        copy.wait_send()


def norm_sum(local, nd, nt):
    lanes = local.shape[1] // (nd * nt)
    x = local.reshape(4, nd, nt, lanes).transpose(2, 1, 0, 3)
    x = jnp.pad(x, ((0, 0), (0, 0), (0, 4), (0, LANES - lanes)))
    vmem = pl.BlockSpec(memory_space=pltpu.VMEM)
    out = pl.pallas_call(
        functools.partial(norm_sum_kernel, nd, nt),
        name="norm_sum",
        out_shape=jax.ShapeDtypeStruct((8, LANES), F32),
        in_specs=[vmem],
        out_specs=vmem,
        scratch_shapes=[
            pltpu.VMEM((nt - 1, nd, 8, LANES), F32),
            pltpu.VMEM((nd, 8, LANES), F32),
            pltpu.VMEM((nd - 1, 8, LANES), F32),
            pltpu.SemaphoreType.DMA((nt - 1,)),
            pltpu.SemaphoreType.DMA((nt - 1,)),
            pltpu.SemaphoreType.DMA((nd - 1,)),
            pltpu.SemaphoreType.DMA((nd - 1,)),
        ],
        compiler_params=pltpu.CompilerParams(collective_id=6, has_side_effects=True),
    )(x)
    return out[:4, :lanes]


def low(values):
    return lax.optimization_barrier(values.astype(BF16)).astype(F32)


def per_device(tokens, w_qkv, w_out, w_up, w_down, norm_gains, norm_biases, lengths, cotangent):
    rows = tokens.shape[0]
    n, nd = lax.axis_size("tensor"), lax.axis_size("dp")
    local_norms = low(jnp.concatenate([norm_gains, norm_biases]))
    local_norms = jnp.pad(local_norms, ((0, 4), (0, 0)))
    normed_one_all, norms = gather_rows(tokens, local_norms, n, nd)
    gains, shifts = norms[:2], norms[2:4]
    qkv_all = lax.all_gather(w_qkv.astype(BF16), "dp", axis=1, tiled=True)
    out_all = lax.all_gather(w_out.astype(BF16), "dp", axis=1, tiled=True)
    up_all = lax.all_gather(w_up.astype(BF16), "dp", axis=0, tiled=True)
    down_all = lax.all_gather(w_down.astype(BF16), "dp", axis=1, tiled=True)
    t = lax.axis_index("tensor")
    heads_local = qkv_all.shape[2] // HEAD_DIM
    head_ids = (t * heads_local + jnp.arange(heads_local, dtype=jnp.int32)).astype(F32)
    slopes = jnp.exp2(-8.0 * (head_ids + 1.0) / (heads_local * n))
    live_rows = (t * rows + jnp.arange(rows, dtype=jnp.int32) < lengths[0])[:, None]
    inputs = tokens.astype(F32)
    hat_one, inv_one = normalize(inputs)
    qkv = project(normed_one_all, qkv_all)
    attn, lse = attend(qkv, slopes, lengths)
    masked_cot = jnp.where(live_rows, cotangent, jnp.zeros_like(cotangent))
    attn_branch, masked_cot_all = branch(attn, out_all, masked_cot, n)
    after_attn = inputs + attn_branch
    hat_two, inv_two = normalize(after_attn)
    normed_two = (hat_two * gains[1] + shifts[1]).astype(BF16)
    normed_two_all, activated, d_up, mlp_part, d_norm_two = feed(
        normed_two, masked_cot_all, up_all, down_all, n
    )
    gain_two = jnp.sum(d_norm_two * hat_two, axis=0)
    shift_two = jnp.sum(d_norm_two, axis=0)
    d_after = masked_cot.astype(F32) + norm_back(d_norm_two, hat_two, inv_two, gains[1])
    d_branch = d_after.astype(BF16)
    grad_down = dot_tn(activated, masked_cot_all).astype(BF16)
    grad_up = dot_tn(normed_two_all, d_up).astype(BF16)
    grad_down, grad_up, d_branch = lax.optimization_barrier((grad_down, grad_up, d_branch))
    down_shard = lax.psum_scatter(grad_down, "dp", scatter_dimension=1, tiled=True)
    up_shard = lax.psum_scatter(grad_up, "dp", scatter_dimension=0, tiled=True)
    passed = unbranch(d_branch, out_all, mlp_part, n)
    passed, down_shard, up_shard = lax.optimization_barrier((passed, down_shard, up_shard))
    d_branch_all, d_attn, mlp_branch = passed
    output = jnp.where(live_rows, after_attn + mlp_branch, 0.0).astype(BF16)
    grad_out = dot_tn(attn, d_branch_all).astype(BF16)
    out_shard = lax.psum_scatter(grad_out, "dp", scatter_dimension=1, tiled=True).astype(F32)
    d_qkv = unattend(qkv, d_attn, lse, slopes, lengths)
    grad_qkv = jnp.stack([dot_tn(normed_one_all, d_qkv[i]) for i in range(3)]).astype(BF16)
    qkv_shard = lax.psum_scatter(grad_qkv, "dp", scatter_dimension=1, tiled=True).astype(F32)
    d_norm_one = unproject(d_qkv, qkv_all, rows, n)
    gain_one = jnp.sum(d_norm_one * hat_one, axis=0)
    shift_one = jnp.sum(d_norm_one, axis=0)
    input_grad = (d_after + norm_back(d_norm_one, hat_one, inv_one, gains[0])).astype(BF16)
    sums = norm_sum(jnp.stack([gain_one, gain_two, shift_one, shift_two]), nd, n)
    return (output, input_grad, qkv_shard, out_shard, up_shard.astype(F32), down_shard.astype(F32), sums[:2], sums[2:])


def solution(mesh):
    placed = (
        P(("dp", "tensor"), None),
        P(None, "dp", "tensor"),
        P("tensor", "dp"),
        P("dp", "tensor"),
        P("tensor", "dp"),
        P(None, "dp"),
        P(None, "dp"),
        P("dp"),
        P(("dp", "tensor"), None),
    )
    return jax.shard_map(
        per_device,
        mesh=mesh,
        in_specs=placed,
        out_specs=(
            P(("dp", "tensor"), None),
            P(("dp", "tensor"), None),
            P(None, "dp", "tensor"),
            P("tensor", "dp"),
            P("dp", "tensor"),
            P("tensor", "dp"),
            P(None, ("dp", "tensor")),
            P(None, ("dp", "tensor")),
        ),
        check_vma=False,
    )
```
